32 devices in a mesh: layer: 4 (over y, x), lat: 8 (over z, core).
Axes of the slice: x: 2, y: 2, z: 4, core: 2. Of those that a mesh axis runs over, the one named last changes fastest.
Arguments:
- inputs: bfloat16 [4, 1, 5120, 128], P(None, None, 'lat'), may hold values from -6 to 6
- encoder: bfloat16 [4, 8192, 5120], P('layer', 'lat'), may hold values from -0.125 to 0.125
- decoder: bfloat16 [4, 4, 8192, 5120], P('layer', None, 'lat'), may hold values from -0.09375 to 0.09375
- encoder_bias: float32 [4, 8192], P(None, 'lat'), may hold values from -3 to 3
- tile_mask: int32 [4, 64, 128], P(None, 'lat'), may hold values 0 or 1
- targets: bfloat16 [1, 5120, 4, 128], P(None, 'lat'), may hold values from -6 to 6
- decoder_bias: float32 [1, 5120, 4], P(None, 'lat'), may hold values from -3 to 3
Outputs:
- errors: bfloat16 [1, 5120, 4, 128], P(None, 'lat')
- input_grads: bfloat16 [4, 5120, 128], P('layer', 'lat')
The draws below stay inside these ranges and needn't reach their ends.
All inputs are finite; a program needn't handle non-finite values. No bound on the sum of `tile_mask` on one device may be relied on, other than what follows from the above.
Results may differ from the reference program's by a relative error of at most 0.0065.
Values may be sent and summed in bfloat16 or wider, within the bound.
A program may use at most 192 MiB of HBM per device.

```python
import jax
import jax.numpy as jnp

D = 5120
F = 8192
LAYERS = 4
TILE = 128
ROWS = 128
QUARTERS = 1


def plant(array, rng, smallest, largest):
    place = [jax.random.randint(jax.random.fold_in(rng, axis), (), 0, length) for axis, length in enumerate(array.shape)]
    main_axis = array.shape.index(max(array.shape))
    neighbour = place[:main_axis] + [(place[main_axis] + 1) % array.shape[main_axis]] + place[main_axis + 1:]
    return array.at[tuple(place)].set(smallest).at[tuple(neighbour)].set(largest)


def raised(drawn, rng, source, target, blocks, factor):
    owner, partner = [(jnp.arange(drawn.shape[dim]) // (drawn.shape[dim] // blocks)).reshape([-1 if axis == dim else 1 for axis in range(drawn.ndim)]) for dim in (source, target)]
    chosen = jax.random.permutation(rng, blocks)[partner]
    strong = (owner == chosen) | (owner == (partner + blocks // 2) % blocks)
    return jnp.where(strong, factor * drawn, drawn)


def shard_levels(stream_key, dims, shards, least, top_value):
    def one(axis_at, blocks):
        steps = jax.random.uniform(jax.random.fold_in(jax.random.fold_in(stream_key, 6), axis_at), (blocks,), jnp.float32, least / len(shards), top_value / len(shards))
        return jnp.repeat(jnp.exp(steps), dims[axis_at] // blocks).reshape((-1,) + (1,) * (len(dims) - axis_at - 1))

    gain = one(*shards[0])
    for cut in shards[1:]:
        gain = gain * one(*cut)
    return gain


def noise(rng, shape, deviation, most, pieces=(), kind=jnp.bfloat16):
    values = deviation * jax.random.normal(rng, shape, jnp.float32)
    if pieces:
        values = values * shard_levels(rng, shape, pieces, -0.22, 0.18)
    return jnp.clip(values, -most, most).astype(kind)


def bell_draw_with(stream_key, extent, width, reach, shards, heavy, dtype=jnp.bfloat16):
    entries = width * jax.random.normal(stream_key, extent, jnp.float32)
    if shards:
        entries = entries * shard_levels(stream_key, extent, shards, -0.22, 0.18)
    return jnp.clip(raised(entries, jax.random.fold_in(stream_key, 3), *heavy), -reach, reach).astype(dtype)


def setup_inputs(seed: int = 0) -> dict:
    keys = jax.random.split(jax.random.key(seed), 8)
    inputs = noise(keys[0], (LAYERS, QUARTERS, D // QUARTERS, ROWS), 1.0, 6.0, ((2, 8),))
    encoder = bell_draw_with(keys[1], (LAYERS * QUARTERS, F, D // QUARTERS), D ** -0.5, 0.125, ((0, 4), (1, 8)), (1, 2, 8, 2.0))
    decoder = bell_draw_with(keys[2], (LAYERS * QUARTERS, LAYERS, F, D // QUARTERS), F ** -0.5, 0.09375, ((0, 4), (2, 8)), (2, 3, 8, 2.0))
    encoder_bias = noise(keys[3], (LAYERS, F), 0.5, 3.0, ((1, 8),), jnp.float32)
    tile_mask = plant((jax.random.randint(keys[4], (LAYERS, F // TILE, ROWS), 0, 4) < 3).astype(jnp.int32), jax.random.fold_in(keys[4], 1), 0, 1)
    targets = noise(keys[5], (QUARTERS, D // QUARTERS, LAYERS, ROWS), 1.0, 6.0, ((1, 8),))
    decoder_bias = noise(keys[6], (QUARTERS, D // QUARTERS, LAYERS), 0.5, 3.0, ((1, 8),), jnp.float32)
    return dict(inputs=inputs, encoder=encoder, decoder=decoder, encoder_bias=encoder_bias, tile_mask=tile_mask, targets=targets, decoder_bias=decoder_bias)


def reference(inputs, encoder, decoder, encoder_bias, tile_mask, targets, decoder_bias):
    layers = inputs.shape[0]
    quarters = inputs.shape[1]
    quarter_width = inputs.shape[2]
    row_count = inputs.shape[3]
    latents = encoder.shape[1]
    enc_blocks = encoder.reshape(layers, quarters, latents, quarter_width)
    dec_blocks = decoder.reshape(layers, quarters, layers, latents, quarter_width)
    support = jnp.repeat(tile_mask.astype(jnp.float32), TILE, axis=1)
    activity = []
    for source in range(layers):
        preacts = jnp.einsum("qfd,qdr->fr", enc_blocks[source].astype(jnp.float32), inputs[source].astype(jnp.float32))
        preacts = preacts + encoder_bias[source][:, None]
        activity.append((jnp.maximum(preacts, 0.0) * support[source]).astype(jnp.bfloat16))
    outputs = []
    for target in range(layers):
        summed = jnp.zeros((quarters, quarter_width, row_count), jnp.float32)
        for source in range(target + 1):
            summed = summed + jnp.einsum("qfd,fr->qdr", dec_blocks[source, :, target].astype(jnp.float32), activity[source].astype(jnp.float32))
        outputs.append(summed)
    stacked = jnp.stack(outputs, axis=2)
    errors = (stacked + decoder_bias[:, :, :, None] - targets.astype(jnp.float32)).astype(jnp.bfloat16)
    gradients = []
    for source in range(layers):
        summed = jnp.zeros((latents, row_count), jnp.float32)
        for target in range(source, layers):
            summed = summed + jnp.einsum("qfd,qdr->fr", dec_blocks[source, :, target].astype(jnp.float32), errors[:, :, target, :].astype(jnp.float32))
        pre_grad = (summed * support[source]).astype(jnp.bfloat16)
        gradients.append(jnp.einsum("qfd,fr->qdr", enc_blocks[source].astype(jnp.float32), pre_grad.astype(jnp.float32)))
    input_grads = jnp.stack(gradients).reshape(layers * quarters, quarter_width, row_count).astype(jnp.bfloat16)
    return errors, input_grads
```

```python
import jax
import jax.numpy as jnp
from jax import lax
from jax.experimental import pallas as pl
from jax.experimental.pallas import tpu as pltpu
from jax.sharding import PartitionSpec as P

TILE = 128


def over_sources(values):
    return lax.psum(values, "layer")


def run_blocks(totals, source_row, blocks, base_target, low_target, high_target, update):

    def advance(target, current):
        weights = lax.dynamic_index_in_dim(blocks, target - base_target, 0, keepdims=False)
        return update(current, target, source_row, weights)

    return lax.fori_loop(low_target, high_target, advance, totals)


def per_device(inputs, encoder, decoder, encoder_bias, tile_mask, targets, decoder_bias):
    layer_count = lax.axis_size("layer")
    lat_count = lax.axis_size("lat")
    layers = decoder.shape[1]
    quarters = layer_count // layers
    position = lax.axis_index("layer")
    source = position // quarters
    quarter = position % quarters
    encoder_rows = encoder[0]
    own_blocks = decoder[0]
    local_latents = encoder_rows.shape[0]
    quarter_width = encoder_rows.shape[1]
    kept_width = quarter_width // lat_count
    row_count = inputs.shape[3]
    block_jobs = [(source, own_blocks, 0, source, layers)]

    def run_all(totals, update):
        block_job = block_jobs[0]
        totals = run_blocks(
            totals, block_job[0], block_job[1], block_job[2], block_job[3], block_job[4], update
        )
        return totals

    own_input = lax.dynamic_index_in_dim(
        inputs.reshape((layers * quarters,) + inputs.shape[2:]), position, 0, keepdims=False
    )
    full_input = lax.all_gather(own_input, "lat", axis=0, tiled=True)
    own_preacts = jnp.dot(encoder_rows, full_input, preferred_element_type=jnp.float32)
    tile_count = tile_mask.shape[1]
    support = jnp.broadcast_to(
        tile_mask[:, :, None, :].astype(jnp.float32), (layers, tile_count, TILE, row_count)
    ).reshape(layers, local_latents, row_count)
    own_support = lax.dynamic_index_in_dim(support, source, 0, keepdims=False)
    source_slots = lax.dynamic_update_index_in_dim(
        jnp.zeros((layers, local_latents, row_count), jnp.float32), own_preacts, source, 0
    )
    preacts = over_sources(source_slots) + encoder_bias[:, :, None]
    activity = (jnp.maximum(preacts, 0.0) * support).astype(jnp.bfloat16)

    def forward_term():

        def update(current, target, source_row, weights):
            latent = lax.dynamic_index_in_dim(activity, source_row, 0, keepdims=False)
            contrib = lax.dot_general(
                weights, latent, (((0,), (0,)), ((), ())), preferred_element_type=jnp.float32
            )
            before = lax.dynamic_index_in_dim(current, target, 1, keepdims=False)
            return lax.dynamic_update_index_in_dim(current, before + contrib, target, 1)

        return run_all(
            jnp.zeros((kept_width * lax.axis_size("lat"), layers, row_count), jnp.float32), update
        )

    partial_value = lax.psum_scatter(forward_term(), "lat", scatter_dimension=0, tiled=True)
    placed = lax.dynamic_update_index_in_dim(
        jnp.zeros((quarters,) + partial_value.shape, jnp.float32), partial_value, quarter, 0
    )
    summed = over_sources(placed)
    errors = (summed + decoder_bias[:, :, :, None] - targets.astype(jnp.float32)).astype(
        jnp.bfloat16
    )
    own_errors = lax.dynamic_index_in_dim(errors, quarter, 0, keepdims=False)

    def fold_errors(totals, portion):

        def update(current, target, source_row, weights):
            error_rows = lax.dynamic_index_in_dim(portion, target, 1, keepdims=False)
            contrib = jnp.dot(weights, error_rows, preferred_element_type=jnp.float32)
            before = lax.dynamic_index_in_dim(current, source_row, 0, keepdims=False)
            return lax.dynamic_update_index_in_dim(current, before + contrib, source_row, 0)

        return run_all(totals, update)

    latent_sums = fold_errors(
        jnp.zeros((layers, local_latents, row_count), jnp.float32),
        lax.all_gather(own_errors, "lat", axis=0, tiled=True),
    )
    latent_grad = over_sources(latent_sums)
    own_latent = lax.dynamic_index_in_dim(latent_grad, source, 0, keepdims=False)
    own_grad = (own_latent * own_support).astype(jnp.bfloat16)
    gradients = lax.psum_scatter(
        lax.dot_general(
            encoder_rows, own_grad, (((0,), (0,)), ((), ())), preferred_element_type=jnp.float32
        ),
        "lat",
        scatter_dimension=0,
        tiled=True,
    )
    return (errors, gradients.astype(jnp.bfloat16)[None])


def width_tile(width):
    tile = width
    while tile > 1280 and tile % 256 == 0:
        tile //= 2
    return tile


def forward_kernel(first_ref, latent_ref, weights_ref, out_ref):
    active = pl.program_id(0) >= first_ref[0]

    @pl.when(active)
    def _():
        term = jnp.dot(latent_ref[...], weights_ref[0], preferred_element_type=jnp.float32)
        out_ref[...] = term.T.astype(out_ref.dtype)

    @pl.when(jnp.logical_not(active))
    def _():
        out_ref[...] = jnp.zeros_like(out_ref)


def spread(first, latent_t, weights, dtype):
    blocks, latents, width = weights.shape
    rows = latent_t.shape[0]
    tile = width_tile(width)
    return pl.pallas_call(
        forward_kernel,
        out_shape=jax.ShapeDtypeStruct((width, blocks * rows), dtype),
        grid_spec=pltpu.PrefetchScalarGridSpec(
            num_scalar_prefetch=1,
            grid=(blocks, width // tile),
            in_specs=[
                pl.BlockSpec((rows, latents), lambda t, d, first: (0, 0)),
                pl.BlockSpec(
                    (1, latents, tile),
                    lambda t, d, first: (
                        jnp.maximum(t, first[0]), 0, jnp.where(t < first[0], 0, d)
                    ),
                ),
            ],
            out_specs=pl.BlockSpec((tile, rows), lambda t, d, first: (d, t)),
        ),
        cost_estimate=pl.CostEstimate(
            flops=2 * blocks * latents * width * rows,
            bytes_accessed=2 * blocks * latents * width,
            transcendentals=0,
        ),
    )(first, latent_t, weights)


def backward_kernel(first_ref, weights_ref, errors_ref, support_ref, out_ref, total):
    target, part = pl.program_id(0), pl.program_id(1)

    @pl.when((target == 0) & (part == 0))
    def _():
        total[...] = jnp.zeros_like(total)

    @pl.when(target >= first_ref[0])
    def _():
        total[...] += jnp.dot(
            weights_ref[0], errors_ref[...], preferred_element_type=jnp.float32
        )

    @pl.when((target == pl.num_programs(0) - 1) & (part == pl.num_programs(1) - 1))
    def _():
        out_ref[...] = (total[...] * support_ref[...]).T.astype(out_ref.dtype)


def gather_back(first, weights, errors, support):
    blocks, latents, width = weights.shape
    rows = support.shape[1]
    tile = width_tile(width)

    def block_of(t, first):
        return jnp.maximum(t, first[0])

    def part_of(t, d, first):
        return jnp.where(t < first[0], 0, d)

    return pl.pallas_call(
        backward_kernel,
        out_shape=jax.ShapeDtypeStruct((rows, latents), jnp.bfloat16),
        grid_spec=pltpu.PrefetchScalarGridSpec(
            num_scalar_prefetch=1,
            grid=(blocks, width // tile),
            in_specs=[
                pl.BlockSpec(
                    (1, latents, tile),
                    lambda t, d, first: (block_of(t, first), 0, part_of(t, d, first)),
                ),
                pl.BlockSpec(
                    (tile, rows),
                    lambda t, d, first: (part_of(t, d, first), block_of(t, first)),
                ),
                pl.BlockSpec((latents, rows), lambda t, d, first: (0, 0)),
            ],
            out_specs=pl.BlockSpec((rows, latents), lambda t, d, first: (0, 0)),
            scratch_shapes=[pltpu.VMEM((latents, rows), jnp.float32)],
        ),
        cost_estimate=pl.CostEstimate(
            flops=2 * blocks * latents * width * rows,
            bytes_accessed=2 * blocks * latents * width,
            transcendentals=0,
        ),
    )(first, weights, errors, support)


def per_device_whole_width(
    inputs, encoder, decoder, encoder_bias, tile_mask, targets, decoder_bias
):
    layers = decoder.shape[1]
    position = lax.axis_index("layer")
    lat = lax.axis_index("lat")
    encoder_rows = encoder[0]
    latents = encoder_rows.shape[0]
    rows = inputs.shape[3]
    kept = targets.shape[1]
    piece = kept // layers
    first = position.astype(jnp.int32)[None]

    def own(values):
        return lax.dynamic_index_in_dim(values, position, 0, keepdims=False)

    full_input = lax.all_gather(own(inputs)[0], "lat", axis=0, tiled=True)
    support = jnp.broadcast_to(
        own(tile_mask)[:, None, :].astype(jnp.float32), (latents // TILE, TILE, rows)
    ).reshape(latents, rows)
    preacts = jnp.dot(encoder_rows, full_input, preferred_element_type=jnp.float32)
    preacts = preacts + own(encoder_bias)[:, None]
    activity_t = (jnp.maximum(preacts, 0.0) * support).astype(jnp.bfloat16).T
    partial_value = spread(first, activity_t, decoder[0], jnp.bfloat16)
    lat_sum = lax.psum_scatter(partial_value, "lat", scatter_dimension=0, tiled=True)
    summed = lax.psum_scatter(
        lat_sum.astype(jnp.float32), "layer", scatter_dimension=0, tiled=True
    ).reshape(piece, layers, rows)
    start = position * piece
    own_targets = lax.dynamic_slice_in_dim(targets[0], start, piece, 0)
    own_bias = lax.dynamic_slice_in_dim(decoder_bias[0], start, piece, 0)
    own_errors = (
        summed + own_bias[:, :, None] - own_targets.astype(jnp.float32)
    ).astype(jnp.bfloat16).reshape(piece, layers * rows)
    full_errors = lax.all_gather(own_errors, ("lat", "layer"), axis=0, tiled=True)
    errors = lax.dynamic_slice_in_dim(full_errors, lat * kept, kept, 0)
    own_grad_t = gather_back(first, decoder[0], full_errors, support)
    gradients = lax.psum_scatter(
        spread(jnp.zeros((1,), jnp.int32), own_grad_t, encoder, jnp.float32),
        "lat",
        scatter_dimension=0,
        tiled=True,
    )
    return (errors.reshape(1, kept, layers, rows), gradients.astype(jnp.bfloat16)[None])


def solution(mesh):
    def run(*arrays):
        if lax.axis_size("layer") == arrays[2].shape[1]:
            return per_device_whole_width(*arrays)
        return per_device(*arrays)

    in_specs = (
        P(None, None, "lat", None),
        P("layer", "lat", None),
        P("layer", None, "lat", None),
        P(None, "lat"),
        P(None, "lat", None),
        P(None, "lat", None, None),
        P(None, "lat", None),
    )
    out_specs = (P(None, "lat", None, None), P("layer", "lat", None))
    return jax.shard_map(
        run, mesh=mesh, in_specs=in_specs, out_specs=out_specs, check_vma=False
    )
```
